256 devices in a mesh: bead: 8 (over y_lo, x), dom: 32 (over y_hi, z, core).
Axes of the slice: x: 4, y: 4 (y_hi: 2, y_lo: 2; y = y_hi * 2 + y_lo), z: 8, core: 2. Of those that a mesh axis runs over, the one named last changes fastest.
Arguments:
- mode_pos: float32 [16, 3, 24576], P('bead', None, 'dom'), may hold values from -6 to 6
- mode_vel: float32 [16, 3, 24576], P('bead', None, 'dom'), may hold values from -6 to 6
- charges: float32 [24576], P('dom'), may hold values from -1.5 to 1.5
Outputs:
- positions: float32 [16, 3, 24576], P('bead', None, 'dom')
- velocities: float32 [16, 3, 24576], P('bead', None, 'dom')
The draws below stay inside these ranges and needn't reach their ends.
All inputs are finite; a program needn't handle non-finite values.
Results may differ from the reference program's by a relative error of at most 0.0003.
Values sent between devices are 32-bit elements; how exact they have to be, the bound alone decides.
No kernel may reach another device: no remote copies, remote signals or barrier semaphores. Data moves between devices by JAX's collectives and lax.ppermute only.
A program may use at most 64 MiB of HBM per device.

```python
import jax
import jax.numpy as jnp
from jax import lax

BEADS = 16
PART_DEV = 768
PARTICLES = 24576
N_DOM = 32


def level_of(own_key, shape, shards, least, top_value):
    def one(dim, shards_of):
        draws = jax.random.uniform(jax.random.fold_in(jax.random.fold_in(own_key, 6), dim), (shards_of,), jnp.float32, least / len(shards), top_value / len(shards))
        return jnp.repeat(jnp.exp(draws), shape[dim] // shards_of).reshape((-1,) + (1,) * (len(shape) - dim - 1))

    loudness = one(*shards[0])
    for cut in shards[1:]:
        loudness = loudness * one(*cut)
    return loudness


def scatter_about(own_key, extent, spread, reach, split=(), kind=jnp.bfloat16):
    factor_of = level_of(own_key, extent, split, -0.22, 0.18) if split else 1.0
    array = jax.random.normal(own_key, extent, jnp.float32) * spread * factor_of
    return jnp.minimum(jnp.maximum(array, -reach), reach).astype(kind)


def setup_inputs(seed: int = 0) -> dict:
    streams_of = jax.random.split(jax.random.key(seed), 4)
    mode_pos = scatter_about(streams_of[0], (BEADS, 3, PARTICLES), 1.0, 6.0, ((0, 8), (2, 32)), jnp.float32)
    mode_vel = scatter_about(streams_of[1], (BEADS, 3, PARTICLES), 1.0, 6.0, ((0, 8), (2, 32)), jnp.float32)
    charges = jnp.clip(jax.random.uniform(streams_of[2], (PARTICLES,), jnp.float32, -1.5, 1.5) * level_of(streams_of[2], (PARTICLES,), ((0, 32),), -0.4, 0.0), -1.5, 1.5)
    return dict(mode_pos=mode_pos, mode_vel=mode_vel, charges=charges)


KAPPA = 2.0
SOFTEN = 0.09
KICK = 0.3
OMEGA = 7.0
STEP_TIME = 0.1
HIGHEST = lax.Precision.HIGHEST

def mode_table(bead_index, mode_index):
    scale_root = jnp.sqrt(jnp.float32(BEADS))
    angle = 2.0 * jnp.pi * bead_index.astype(jnp.float32) * mode_index.astype(jnp.float32) / BEADS
    first = jnp.ones_like(angle) / scale_root
    middle = jnp.cos(jnp.pi * bead_index.astype(jnp.float32)) / scale_root + 0.0 * angle
    factor = jnp.sqrt(2.0 / jnp.float32(BEADS))
    return jnp.where(mode_index == 0, first, jnp.where(2 * mode_index < BEADS, factor * jnp.cos(angle), jnp.where(2 * mode_index == BEADS, middle, factor * jnp.sin(angle))))

def evolve(mode_pos, mode_vel, mode_index):
    freq = 2.0 * OMEGA * jnp.sin(jnp.pi * mode_index.astype(jnp.float32) / BEADS)
    theta = freq * STEP_TIME
    cosine = jnp.cos(theta)[:, None, None]
    sine = jnp.sin(theta)
    safe_freq = jnp.where(mode_index > 0, freq, 1.0)
    carry_rate = jnp.where(mode_index > 0, sine / safe_freq, STEP_TIME)[:, None, None]
    new_pos = cosine * mode_pos + carry_rate * mode_vel
    new_vel = (-freq * sine)[:, None, None] * mode_pos + cosine * mode_vel
    return (new_pos, new_vel)

def pair_force(near_pos, near_charge, far_pos, far_charge):
    delta = near_pos[:, :, :, None] - far_pos[:, :, None, :]
    square = lax.optimization_barrier(jnp.sum(delta * delta, axis=1)) + SOFTEN
    distance = jnp.sqrt(square)
    weight = near_charge[None, :, None] * far_charge[None, None, :] * jnp.exp(-KAPPA * distance) * (1.0 + KAPPA * distance) / (square * distance)
    return lax.optimization_barrier(jnp.sum(weight[:, None] * delta, axis=3))

def reference(mode_pos, mode_vel, charges):
    modes = jnp.arange(BEADS, dtype=jnp.int32)
    new_pos, new_vel = evolve(mode_pos, mode_vel, modes)
    table = mode_table(modes[:, None], modes[None, :])
    positions = jnp.einsum('bk,kcn->bcn', table, new_pos, precision=HIGHEST)
    bead_vel = jnp.einsum('bk,kcn->bcn', table, new_vel, precision=HIGHEST)

    def bead_force(bead_pos):
        whole = bead_pos[None]

        def one_block(block_index):
            start = (block_index * PART_DEV).astype(jnp.int32)
            near = lax.dynamic_slice_in_dim(whole, start, PART_DEV, 2)
            near_charge = lax.dynamic_slice_in_dim(charges, start, PART_DEV, 0)
            return pair_force(near, near_charge, whole, charges)[0]
        blocks = lax.map(one_block, jnp.arange(N_DOM, dtype=jnp.int32))
        return jnp.transpose(blocks, (1, 0, 2)).reshape(3, PARTICLES)
    forces = lax.map(bead_force, positions)
    return (positions, bead_vel + KICK * forces)
```

```python
import functools
import math

import jax
import jax.numpy as jnp
import numpy as np
from jax import lax
from jax.experimental import pallas as pl
from jax.experimental.pallas import tpu as pltpu
from jax.sharding import PartitionSpec as P

BEADS = 16
KAPPA = 2.0
SOFTEN = 0.09
KICK = 0.3
OMEGA = 7.0
STEP_TIME = 0.1
LN2 = math.log(2.0)
ALPHA = KAPPA / LN2
F32 = jnp.float32
BF = jnp.bfloat16
ROWS = 256


HELD = ((0, 0, 0), (0, 0, 1), (0, 1, 1), (1, 0, 0), (2, 0, 0), (4, 1, 0), (5, 0, 0))
PEERS = ((0, 0), (1, 0), (3, 0), (0, 1), (1, 1), (3, 1), (2, 0), (2, 1))


def dom_shift(dom, offset):
    z, core, y = (dom // 2) % 8, dom % 2, dom // 16
    return (y ^ offset[2]) * 16 + ((z + offset[0]) % 8) * 2 + (core ^ offset[1])


def bead_shift(bead, offset):
    x, y = bead % 4, bead // 4
    return (y ^ offset[1]) * 4 + (x + offset[0]) % 4


def mode_table():
    b, k = np.meshgrid(np.arange(BEADS), np.arange(BEADS), indexing="ij")
    angle = 2.0 * np.pi * ((b * k) % BEADS) / BEADS
    wave = np.sqrt(2.0 / BEADS) * np.where(2 * k < BEADS, np.cos(angle), np.sin(angle))
    edge = np.where(k == 0, 1.0, np.cos(np.pi * b)) / np.sqrt(BEADS)
    return np.where((k == 0) | (2 * k == BEADS), edge, wave)


def evolve_table():
    k = np.arange(BEADS)
    freq = 2.0 * OMEGA * np.sin(np.pi * k / BEADS)
    theta = freq * STEP_TIME
    rate = np.where(k > 0, np.sin(theta) / np.where(k > 0, freq, 1.0), STEP_TIME)
    return np.stack([np.cos(theta), rate, -freq * np.sin(theta), np.cos(theta)], axis=1)


def mix_table():
    table = mode_table()
    out = np.zeros((8, len(PEERS), 2, 2))
    for p in range(8):
        for r, offset in enumerate(PEERS):
            q = bead_shift(p, offset)
            out[p, r] = table[2 * p : 2 * p + 2, 2 * q : 2 * q + 2]
    return out.reshape(-1).astype(np.float32)


def tile_list():
    tiles = [(0, 0, 0, 0), (0, 0, 1, 0)]
    seen = {(0, 0, 0)}
    for b in range(len(HELD)):
        for a in range(b):
            u, v = HELD[a], HELD[b]
            d = ((v[0] - u[0]) % 8, v[1] ^ u[1], v[2] ^ u[2])
            n = ((-d[0]) % 8, d[1], d[2])
            if d in seen:
                continue
            seen.update((d, n))
            if d == n:
                tiles.append((a, b, 0, 1 if d[1] else 2 if d[2] else 3))
            else:
                tiles += [(a, b, 0, 0), (a, b, 1, 0)]
    assert len(seen) == 32
    return tiles


def chunk_table(count):
    spare = 2 * len(HELD)
    idle = (0, 0, 0, spare, spare, 0)
    rows = [idle, idle]
    for a, b, bead, bit in tile_list():
        a, b, diagonal = 2 * a + bead, 2 * b + bead, a == b
        for first in range(0, count, ROWS):
            rows.append((a, b, first, a, spare if diagonal else b, bit))
    trips = (len(rows) + 1) // 2
    rows += [idle] * (2 * trips + 2 - len(rows))
    return np.array(rows, np.int32).T.copy(), trips


def dot(left, right):
    return lax.dot_general(left, right, (((1,), (0,)), ((), ())), preferred_element_type=F32)


def split3(x):
    first = x.astype(BF).astype(F32)
    rest = x - first
    second = rest.astype(BF).astype(F32)
    return first, second, rest - second


def evolve_kernel(where, table, pos, vel, out):
    base = where[0] * 8
    for m in range(2):
        c0, c1, c2, c3 = (table[base + 4 * m + i] for i in range(4))
        p, v = pos[m], vel[m]
        out[m, 0:3] = c0 * p + c1 * v
        out[m, 3:6] = c2 * p + c3 * v


def mix_kernel(where, table, *refs):
    pieces, charges, (pos, vel, pack) = refs[: len(PEERS)], refs[len(PEERS)], refs[len(PEERS) + 1 :]
    base = where[0] * (4 * len(PEERS))
    for b in range(2):
        total = None
        for r in range(len(PEERS)):
            for m in range(2):
                term = table[base + 4 * r + 2 * b + m] * pieces[r][m]
                total = term if total is None else total + term
        pos[b] = total[0:3]
        vel[b] = total[3:6]
        pack[b, 0:3] = total[0:3]
        pack[b, 3:4] = charges[...]


def operands(pack):
    count = pack.shape[1]
    x = pack[0:3] * ALPHA
    q = pack[3:4]
    x1, x2, x3 = split3(x)
    n1, n2, n3 = split3(jnp.sum(x * x, axis=0, keepdims=True) + 0.5 * SOFTEN * ALPHA * ALPHA)
    one = jnp.ones((1, count), F32)
    pad = jnp.zeros((8, count), F32)
    far = jnp.concatenate([n1, n2, n3, one, one, one, -2 * x1, -2 * x1, -2 * x2, -2 * x2, -2 * x1, -2 * x3, pad], axis=0)
    near = jnp.concatenate([one, one, one, n1, n2, n3, x1, x2, x1, x2, x3, x1, pad], axis=0)
    v1, v2, v3 = split3(jnp.concatenate([x * q, q], axis=0))
    source = jnp.concatenate([v1, v2, v3, jnp.zeros((4, count), F32)], axis=0)
    return far, near, source


def pair_kernel(trips, tab, bits, *refs):
    held = len(HELD)
    packs, outs = refs[:held], refs[held : 2 * held]
    far, near, source, sums, s0, s1, h0, h1, t0, t1 = refs[2 * held :]
    count = packs[0].shape[2]
    for i in range(held):

        def prepare(b, carry, i=i):
            l, r, v = operands(packs[i][b])
            far[2 * i + b] = l.T.astype(BF)
            near[2 * i + b] = r.astype(BF)
            source[2 * i + b] = v.astype(BF)
            sums[2 * i + b] = jnp.zeros((16, count), F32)
            return carry

        lax.fori_loop(0, 2, prepare, 0)
    sums[2 * held] = jnp.zeros((16, count), F32)
    s0[...] = jnp.ones_like(s0)
    s1[...] = jnp.ones_like(s1)
    for x in (h0, h1, t0, t1):
        x[...] = jnp.zeros_like(x)
    dist, weight, turned = (s0, s1), (h0, h1), (t0, t1)

    def step(trip, carry):
        for u in (0, 1):
            k = 2 * trip + u
            bit = bits[tab[5, k]]
            a, b, row = tab[0, k] + bit, tab[1, k] + bit, pl.multiple_of(tab[2, k], ROWS)
            sum_a, sum_b = tab[3, k] + bit, tab[4, k] + bit
            bit = bits[tab[5, k + 2]]
            next_a, next_b, next_row = tab[0, k + 2] + bit, tab[1, k + 2] + bit, pl.multiple_of(tab[2, k + 2], ROWS)
            source_a, source_b = source[a], source[b, :, pl.ds(row, ROWS)]
            next_far = far[next_b, pl.ds(next_row, ROWS), :]
            react = None
            for first in range(0, count, 256):
                c = slice(first, first + 256)
                old, new = 1 - u, u
                sums[sum_a, :, c] += dot(source_b, weight[old][0, :, c]) + dot(source_b, weight[old][1, :, c])
                part = dot(source_a[:, c], turned[old][0, c, :]) + dot(source_a[:, c], turned[old][1, c, :])
                react = part if react is None else react + part
                dist[new][:, c] = dot(next_far, near[next_a, :, c])
                s = dist[old][:, c]
                y = lax.rsqrt(s)
                g = (jnp.exp2(-(s * y)) * (y * y)) * (y + LN2)
                high = g.astype(BF)
                low = (g - high.astype(F32)).astype(BF)
                weight[new][0, :, c] = high
                weight[new][1, :, c] = low
                turned[new][0, c, :] = high.T
                turned[new][1, c, :] = low.T
            sums[sum_b, :, pl.ds(row, ROWS)] += react
        return carry

    lax.fori_loop(0, trips, step, 0)
    for i in range(held):

        def finish(b, carry, i=i):
            f = sums[2 * i + b]
            f = f[0:4] + f[4:8] + f[8:12]
            pack = packs[i][b]
            outs[i][b] = (pack[0:3] * ALPHA * f[3:4] - f[0:3]) * (pack[3:4] * (KICK * ALPHA * ALPHA))
            return carry

        lax.fori_loop(0, 2, finish, 0)


VM = pl.BlockSpec(memory_space=pltpu.VMEM)
SM = pl.BlockSpec(memory_space=pltpu.SMEM)


def local(mode_pos, mode_vel, charges):
    count = mode_pos.shape[2]
    bead = lax.axis_index("bead").astype(jnp.int32)
    dom = lax.axis_index("dom").astype(jnp.int32)
    where = bead.reshape(1)
    evolved = pl.pallas_call(
        evolve_kernel,
        out_shape=jax.ShapeDtypeStruct((2, 6, count), F32),
        in_specs=[SM, SM, VM, VM],
        out_specs=VM,
        name="evolve",
    )(where, jnp.asarray(evolve_table().reshape(-1).astype(np.float32)), mode_pos, mode_vel)
    pieces = [evolved]
    for offset in PEERS[1:]:
        pieces.append(lax.ppermute(evolved, "bead", [(bead_shift(d, offset), d) for d in range(8)]))
    pos, vel, pack = pl.pallas_call(
        mix_kernel,
        out_shape=(
            jax.ShapeDtypeStruct((2, 3, count), F32),
            jax.ShapeDtypeStruct((2, 3, count), F32),
            jax.ShapeDtypeStruct((2, 4, count), F32),
        ),
        in_specs=[SM, SM] + [VM] * (len(PEERS) + 1),
        out_specs=(VM, VM, VM),
        name="mix",
    )(where, jnp.asarray(mix_table()), *pieces, charges.reshape(1, count))
    packs = [pack]
    for offset in HELD[1:]:
        packs.append(lax.ppermute(pack, "dom", [(dom_shift(d, offset), d) for d in range(32)]))
    table, trips = chunk_table(count)
    held = len(HELD)
    bits = jnp.stack([jnp.int32(0), dom % 2, dom // 16, (dom // 8) % 2])
    forces = pl.pallas_call(
        functools.partial(pair_kernel, trips),
        out_shape=tuple(jax.ShapeDtypeStruct((2, 3, count), F32) for _ in range(held)),
        in_specs=[SM, SM] + [VM] * held,
        out_specs=(VM,) * held,
        scratch_shapes=[
            pltpu.VMEM((2 * held, count, 32), BF),
            pltpu.VMEM((2 * held, 32, count), BF),
            pltpu.VMEM((2 * held, 16, count), BF),
            pltpu.VMEM((2 * held + 1, 16, count), F32),
            pltpu.VMEM((ROWS, count), F32),
            pltpu.VMEM((ROWS, count), F32),
            pltpu.VMEM((2, ROWS, count), BF),
            pltpu.VMEM((2, ROWS, count), BF),
            pltpu.VMEM((2, count, ROWS), BF),
            pltpu.VMEM((2, count, ROWS), BF),
        ],
        name="pair_force",
    )(jnp.asarray(table), bits, *packs)
    total = vel + forces[0]
    for offset, force in zip(HELD[1:], forces[1:]):
        total = total + lax.ppermute(force, "dom", [(d, dom_shift(d, offset)) for d in range(32)])
    return (pos, total)


def solution(mesh):
    placed = (P("bead", None, "dom"), P("bead", None, "dom"), P("dom"))
    return jax.shard_map(
        local,
        mesh=mesh,
        in_specs=placed,
        out_specs=(P("bead", None, "dom"), P("bead", None, "dom")),
        check_vma=False,
    )
```

```python
import functools
import math

import jax
import jax.numpy as jnp
import numpy as np
from jax import lax
from jax.experimental import pallas as pl
from jax.experimental.pallas import tpu as pltpu
from jax.sharding import PartitionSpec as P

BEADS = 16
KAPPA = 2.0
SOFTEN = 0.09
KICK = 0.3
OMEGA = 7.0
STEP_TIME = 0.1
LN2 = math.log(2.0)
ALPHA = KAPPA / LN2
F32 = jnp.float32
BF = jnp.bfloat16
ROWS = 256


HELD = ((0, 0, 0), (0, 0, 1), (0, 1, 1), (1, 0, 0), (2, 0, 0), (4, 1, 0), (5, 0, 0))
RING = (0, 1, 3, 2)
PEERS = tuple((x, y) for x in RING for y in (0, 1))
UNROLL = 6


def dom_shift(dom, offset):
    z, core, y = (dom // 2) % 8, dom % 2, dom // 16
    return (y ^ offset[2]) * 16 + ((z + offset[0]) % 8) * 2 + (core ^ offset[1])


def bead_shift(bead, offset):
    x, y = bead % 4, bead // 4
    return (y ^ offset[1]) * 4 + (x + offset[0]) % 4


def mode_table():
    b, k = np.meshgrid(np.arange(BEADS), np.arange(BEADS), indexing="ij")
    angle = 2.0 * np.pi * ((b * k) % BEADS) / BEADS
    wave = np.sqrt(2.0 / BEADS) * np.where(2 * k < BEADS, np.cos(angle), np.sin(angle))
    edge = np.where(k == 0, 1.0, np.cos(np.pi * b)) / np.sqrt(BEADS)
    return np.where((k == 0) | (2 * k == BEADS), edge, wave)


def evolve_table():
    k = np.arange(BEADS)
    freq = 2.0 * OMEGA * np.sin(np.pi * k / BEADS)
    theta = freq * STEP_TIME
    rate = np.where(k > 0, np.sin(theta) / np.where(k > 0, freq, 1.0), STEP_TIME)
    return np.stack([np.cos(theta), rate, -freq * np.sin(theta), np.cos(theta)], axis=1)


def mix_table():
    table = mode_table()
    out = np.zeros((8, len(PEERS), 2, 2))
    for p in range(8):
        for r, offset in enumerate(PEERS):
            q = bead_shift(p, offset)
            out[p, r] = table[2 * p : 2 * p + 2, 2 * q : 2 * q + 2]
    return out.reshape(-1).astype(np.float32)


def tile_list():
    tiles = [(0, 0, 0, 0), (0, 0, 1, 0)]
    seen = {(0, 0, 0)}
    for b in range(len(HELD)):
        for a in range(b):
            u, v = HELD[a], HELD[b]
            d = ((v[0] - u[0]) % 8, v[1] ^ u[1], v[2] ^ u[2])
            n = ((-d[0]) % 8, d[1], d[2])
            if d in seen:
                continue
            seen.update((d, n))
            if d == n:
                tiles.append((a, b, 0, 1 if d[1] else 2 if d[2] else 3))
            else:
                tiles += [(a, b, 0, 0), (a, b, 1, 0)]
    assert len(seen) == 32
    return tiles


def chunk_table(count):
    spare = 2 * len(HELD)
    idle = (0, 0, 0, spare, spare, 0)
    rows = [idle, idle]
    for a, b, bead, bit in tile_list():
        a, b, diagonal = 2 * a + bead, 2 * b + bead, a == b
        for first in range(0, count, ROWS):
            rows.append((a, b, first, a, spare if diagonal else b, bit))
    trips = -(-len(rows) // UNROLL)
    rows += [idle] * (UNROLL * trips + 2 - len(rows))
    return np.array(rows, np.int32).T.copy(), trips


def dot(left, right):
    return lax.dot_general(left, right, (((1,), (0,)), ((), ())), preferred_element_type=F32)


def split3(x):
    first = x.astype(BF).astype(F32)
    rest = x - first
    second = rest.astype(BF).astype(F32)
    return first, second, rest - second


def by_mode(first, second):
    mode = lax.broadcasted_iota(jnp.int32, (1, 2, 1), 1)
    return jnp.where(mode == 0, first, second)


def evolve_kernel(where, table, pos, vel, out):
    base = where[0] * 8
    c0, c1, c2, c3 = (by_mode(table[base + i], table[base + 4 + i]) for i in range(4))
    p, v = pos[...], vel[...]
    out[0:3] = c0 * p + c1 * v
    out[3:6] = c2 * p + c3 * v


def mix_kernel(where, table, *refs):
    pieces, charges, (pos, vel, pack) = refs[: len(RING)], refs[len(RING)], refs[len(RING) + 1 :]
    base = where[0] * (4 * len(PEERS))
    for b in range(2):
        total = None
        for r in range(len(PEERS)):
            at = base + 4 * r + 2 * b
            term = by_mode(table[at], table[at + 1]) * pieces[r // 2][6 * (r % 2) : 6 * (r % 2) + 6]
            total = term if total is None else total + term
        total = total[:, 0] + total[:, 1]
        pos[:, b] = total[0:3]
        vel[:, b] = total[3:6]
        pack[b, 0:3] = total[0:3]
        pack[b, 3:4] = charges[...].reshape(1, -1)


def operands(pack):
    count = pack.shape[1]
    x = pack[0:3] * ALPHA
    q = pack[3:4]
    x1, x2, x3 = split3(x)
    n1, n2, n3 = split3(jnp.sum(x * x, axis=0, keepdims=True) + 0.5 * SOFTEN * ALPHA * ALPHA)
    one = jnp.ones((1, count), F32)
    pad = jnp.zeros((8, count), F32)
    far = jnp.concatenate([n1, n2, n3, one, one, one, -2 * x1, -2 * x1, -2 * x2, -2 * x2, -2 * x1, -2 * x3, pad], axis=0)
    near = jnp.concatenate([one, one, one, n1, n2, n3, x1, x2, x1, x2, x3, x1, pad], axis=0)
    v1, v2, v3 = split3(jnp.concatenate([x * q, q], axis=0))
    source = jnp.concatenate([v1, v2, v3, jnp.zeros((4, count), F32)], axis=0)
    return far, near, source


def pair_kernel(trips, tab, bits, *refs):
    held = len(HELD)
    packs, outs = refs[:held], refs[held : 2 * held]
    far, near, source, sums, s0, s1, h0, h1, t0, t1 = refs[2 * held :]
    count = packs[0].shape[2]
    for i in range(held):

        def prepare(b, carry, i=i):
            l, r, v = operands(packs[i][b])
            far[2 * i + b] = l.T.astype(BF)
            near[2 * i + b] = r.astype(BF)
            source[2 * i + b] = v.astype(BF)
            sums[2 * i + b] = jnp.zeros((16, count), F32)
            return carry

        lax.fori_loop(0, 2, prepare, 0)
    sums[2 * held] = jnp.zeros((16, count), F32)
    s0[...] = jnp.ones_like(s0)
    s1[...] = jnp.ones_like(s1)
    for x in (h0, h1, t0, t1):
        x[...] = jnp.zeros_like(x)
    dist, weight, turned = (s0, s1), (h0, h1), (t0, t1)

    def step(trip, carry):
        for i in range(UNROLL):
            k, u = UNROLL * trip + i, i % 2
            bit = bits[tab[5, k]]
            a, b, row = tab[0, k] + bit, tab[1, k] + bit, pl.multiple_of(tab[2, k], ROWS)
            sum_a, sum_b = tab[3, k] + bit, tab[4, k] + bit
            bit = bits[tab[5, k + 2]]
            next_a, next_b, next_row = tab[0, k + 2] + bit, tab[1, k + 2] + bit, pl.multiple_of(tab[2, k + 2], ROWS)
            source_a, source_b = source[a], source[b, :, pl.ds(row, ROWS)]
            next_far = far[next_b, pl.ds(next_row, ROWS), :]
            react = None
            for first in range(0, count, 256):
                c = slice(first, first + 256)
                old, new = 1 - u, u
                sums[sum_a, :, c] += dot(source_b, weight[old][0, :, c]) + dot(source_b, weight[old][1, :, c])
                part = dot(source_a[:, c], turned[old][0, c, :]) + dot(source_a[:, c], turned[old][1, c, :])
                react = part if react is None else react + part
                dist[new][:, c] = dot(next_far, near[next_a, :, c])
                s = dist[old][:, c]
                y = lax.rsqrt(s)
                g = (jnp.exp2(-(s * y)) * (y * y)) * (y + LN2)
                high = g.astype(BF)
                low = (g - high.astype(F32)).astype(BF)
                weight[new][0, :, c] = high
                weight[new][1, :, c] = low
                turned[new][0, c, :] = high.T
                turned[new][1, c, :] = low.T
            sums[sum_b, :, pl.ds(row, ROWS)] += react
        return carry

    lax.fori_loop(0, trips, step, 0)
    for i in range(held):
        for b in range(2):
            f = sums[2 * i + b]
            f = f[0:4] + f[4:8] + f[8:12]
            pack = packs[i][b]
            outs[i][:, b] = (pack[0:3] * ALPHA * f[3:4] - f[0:3]) * (pack[3:4] * (KICK * ALPHA * ALPHA))


VM = pl.BlockSpec(memory_space=pltpu.VMEM)
SM = pl.BlockSpec(memory_space=pltpu.SMEM)


def local(mode_pos, mode_vel, charges):
    count = mode_pos.shape[2]
    bead = lax.axis_index("bead").astype(jnp.int32)
    dom = lax.axis_index("dom").astype(jnp.int32)
    where = bead.reshape(1)
    evolved = pl.pallas_call(
        evolve_kernel,
        out_shape=jax.ShapeDtypeStruct((6, 2, count), F32),
        in_specs=[SM, SM, VM, VM],
        out_specs=VM,
        name="evolve",
    )(
        where,
        jnp.asarray(evolve_table().reshape(-1).astype(np.float32)),
        jnp.transpose(mode_pos, (1, 0, 2)),
        jnp.transpose(mode_vel, (1, 0, 2)),
    )
    beside = lax.ppermute(evolved, "bead", [(bead_shift(d, (0, 1)), d) for d in range(8)])
    joined = jnp.concatenate([evolved, beside], axis=0)
    pieces = [joined]
    for x in RING[1:]:
        pieces.append(lax.ppermute(joined, "bead", [(bead_shift(d, (x, 0)), d) for d in range(8)]))
    pos, vel, pack = pl.pallas_call(
        mix_kernel,
        out_shape=(
            jax.ShapeDtypeStruct((3, 2, count), F32),
            jax.ShapeDtypeStruct((3, 2, count), F32),
            jax.ShapeDtypeStruct((2, 4, count), F32),
        ),
        in_specs=[SM, SM] + [VM] * (len(RING) + 1),
        out_specs=(VM, VM, VM),
        name="mix",
    )(where, jnp.asarray(mix_table()), *pieces, charges)
    packs = [pack]
    for offset in HELD[1:]:
        packs.append(lax.ppermute(pack, "dom", [(dom_shift(d, offset), d) for d in range(32)]))
    table, trips = chunk_table(count)
    held = len(HELD)
    bits = jnp.stack([jnp.int32(0), dom % 2, dom // 16, (dom // 8) % 2])
    forces = pl.pallas_call(
        functools.partial(pair_kernel, trips),
        out_shape=tuple(jax.ShapeDtypeStruct((3, 2, count), F32) for _ in range(held)),
        in_specs=[SM, SM] + [VM] * held,
        out_specs=(VM,) * held,
        scratch_shapes=[
            pltpu.VMEM((2 * held, count, 32), BF),
            pltpu.VMEM((2 * held, 32, count), BF),
            pltpu.VMEM((2 * held, 16, count), BF),
            pltpu.VMEM((2 * held + 1, 16, count), F32),
            pltpu.VMEM((ROWS, count), F32),
            pltpu.VMEM((ROWS, count), F32),
            pltpu.VMEM((2, ROWS, count), BF),
            pltpu.VMEM((2, ROWS, count), BF),
            pltpu.VMEM((2, count, ROWS), BF),
            pltpu.VMEM((2, count, ROWS), BF),
        ],
        name="pair_force",
    )(jnp.asarray(table), bits, *packs)
    total = vel + forces[0]
    for offset, force in zip(HELD[1:], forces[1:]):
        total = total + lax.ppermute(force, "dom", [(d, dom_shift(d, offset)) for d in range(32)])
    return (jnp.transpose(pos, (1, 0, 2)), jnp.transpose(total, (1, 0, 2)))


def solution(mesh):
    placed = (P("bead", None, "dom"), P("bead", None, "dom"), P("dom"))
    return jax.shard_map(
        local,
        mesh=mesh,
        in_specs=placed,
        out_specs=(P("bead", None, "dom"), P("bead", None, "dom")),
        check_vma=False,
    )
```
